32 devices in a mesh: groups: 2 (over y), seq: 4 (over z), tile: 2 (over x), chan: 2 (over core).
Axes of the slice: x: 2, y: 2, z: 4, core: 2. Of those that a mesh axis runs over, the one named last changes fastest.
Arguments:
- latents: bfloat16 [2, 7680, 384], P('tile', ('groups', 'seq'), 'chan'), parts along dimension 1, may hold values from -6 to 6
- norm_gain: float32 [384], replicated, may hold values from 0.1 to 1.9
- conv_weight: bfloat16 [3, 3, 3, 384, 384], P(None, None, None, None, 'chan'), may hold values from -0.0625 to 0.0625
- conv_bias: float32 [384], P('chan'), may hold values from -3 to 3
- upsample_weight: bfloat16 [3, 3, 384, 192], P(None, None, None, 'chan'), may hold values from -0.109375 to 0.109375
- upsample_bias: float32 [192], P('chan'), may hold values from -3 to 3
Outputs:
- decoded: bfloat16 [8, 192, 20, 384], P(None, ('groups', 'tile'), 'seq', 'chan'), parts along dimension 1
The draws below stay inside these ranges and needn't reach their ends.
There are 2 independent parts, one for each index of `groups`. The reference program is written for one: setup_inputs(seed, part) draws one part's arguments, and reference() takes and returns one part's arrays. A program takes and returns all parts, laid end to end along the dimension named above; an argument that names none is the same for every part. Nothing has to cross between parts.
All inputs are finite; a program needn't handle non-finite values.
Results may differ from the reference program's by a relative error of at most 0.005.
Values may be sent and summed in bfloat16 or wider, within the bound.
No kernel may reach another device: no remote copies, remote signals or barrier semaphores. Data moves between devices by JAX's collectives and lax.ppermute only.
A program may use at most 64 MiB of HBM per device.

```python
import jax
import jax.numpy as jnp
from jax import lax

C = 384
CO = 192
FRAMES = 8
ROWS_DEV = 24
BLOCKS = 2
H = 48
W = 20
TOKQ = 3840


def block_levels(own_key, shape, pieces, low, largest):
    gain, own = 1.0, jax.random.fold_in(own_key, 6)
    for dim, parts in pieces:
        draws = jnp.exp(jax.random.uniform(jax.random.fold_in(own, dim), (parts,), jnp.float32, low / len(pieces), largest / len(pieces)))
        gain = gain * jnp.repeat(draws, shape[dim] // parts).reshape([-1 if axis == dim else 1 for axis in range(len(shape))])
    return gain


def centred(own_key, dims, scale, reach, cuts=(), held_as=jnp.bfloat16):
    entries = scale * jax.random.normal(own_key, dims, jnp.float32)
    if cuts:
        entries = entries * block_levels(own_key, dims, cuts, -0.22, 0.18)
    return jnp.clip(entries, -reach, reach).astype(held_as)


def setup_inputs(seed: int = 0, part: int = 0) -> dict:
    streams_of = jax.random.split(jax.random.key(seed), 7)
    own_keys = jax.random.split(jax.random.fold_in(streams_of[6], part), 7)
    latents = centred(own_keys[0], (BLOCKS, TOKQ, C), 1.0, 6.0, ((0, 2), (1, 4), (2, 2)))
    norm_gain = jnp.clip(1.0 + 0.18 * jax.random.normal(streams_of[1], (C,), jnp.float32), 0.1, 1.9)
    conv_weight = centred(streams_of[2], (3, 3, 3, C, C), (27 * C) ** -0.5, 0.0625, ((4, 2),))
    conv_bias = centred(streams_of[3], (C,), 0.5, 3.0, ((0, 2),), jnp.float32)
    upsample_weight = centred(streams_of[4], (3, 3, C, CO), (9 * C) ** -0.5, 0.109375, ((3, 2),))
    upsample_bias = centred(streams_of[5], (CO,), 0.5, 3.0, ((0, 2),), jnp.float32)
    return dict(latents=latents, norm_gain=norm_gain, conv_weight=conv_weight, conv_bias=conv_bias, upsample_weight=upsample_weight, upsample_bias=upsample_bias)


def reference(latents, norm_gain, conv_weight, conv_bias, upsample_weight, upsample_bias):
    field = latents.reshape(BLOCKS, FRAMES, ROWS_DEV, W, C)
    field = jnp.transpose(field, (1, 0, 2, 3, 4)).reshape(FRAMES, H, W, C)
    values = field.astype(jnp.float32)
    scale = lax.rsqrt(lax.optimization_barrier(jnp.mean(values * values, axis=-1, keepdims=True)) + 1e-06)
    act = jax.nn.silu(values * scale * norm_gain).astype(jnp.bfloat16)
    padded = jnp.pad(act, ((2, 0), (1, 1), (1, 1), (0, 0)))
    conv = lax.conv_general_dilated(padded[None], conv_weight, (1, 1, 1), 'VALID', dimension_numbers=('NDHWC', 'DHWIO', 'NDHWC'), preferred_element_type=jnp.float32)[0]
    middle = (field.astype(jnp.float32) + conv + conv_bias).astype(jnp.bfloat16)
    upsampled = jnp.repeat(jnp.repeat(middle, 2, axis=1), 2, axis=2)
    upsampled = jnp.pad(upsampled, ((0, 0), (1, 1), (1, 1), (0, 0)))
    image = lax.conv_general_dilated(upsampled, upsample_weight, (1, 1), 'VALID', dimension_numbers=('NHWC', 'HWIO', 'NHWC'), preferred_element_type=jnp.float32)
    image = image + upsample_bias
    image = image.reshape(FRAMES, 2 * H, W, 2, CO)
    image = jnp.transpose(image, (0, 1, 2, 4, 3)).reshape(FRAMES, 2 * H, W, 2 * CO)
    return image.astype(jnp.bfloat16)
```

```python
import functools

import jax
import jax.numpy as jnp
from jax import lax
from jax.experimental import pallas as pl
from jax.experimental.pallas import tpu as pltpu
from jax.sharding import PartitionSpec as P

FRAMES = 8
ROWS_DEV = 24
PAIRS = FRAMES // 2
PITCH = 32
HEAD = 8

norm_eps = 1e-06
f32 = jnp.float32
bf16 = jnp.bfloat16
VM = pl.BlockSpec(memory_space=pltpu.VMEM)
ANY = pl.BlockSpec(memory_space=pl.ANY)
MIB = 1024 * 1024


def dot_nt(a, b):
    return lax.dot_general(a, b, (((1,), (1,)), ((), ())), preferred_element_type=f32)


def call(kernel, out_shape, in_specs, out_specs, scratch, limit, name, flops=0, moved=0, aliases=None):
    return pl.pallas_call(
        kernel,
        out_shape=out_shape,
        in_specs=in_specs,
        out_specs=out_specs,
        scratch_shapes=list(scratch),
        compiler_params=pltpu.CompilerParams(vmem_limit_bytes=limit * MIB),
        input_output_aliases=aliases or {},
        cost_estimate=pl.CostEstimate(flops=flops, bytes_accessed=moved, transcendentals=0),
        name=name,
    )


def round_up(n, k):
    return -(-n // k) * k


def border_rows(width):
    return round_up(2 * width, 8)


def edge_kernel(span, colors, x_ref, *outs):
    tile = lax.axis_index("tile")
    half = ROWS_DEV * span
    seg = round_up(2 * span, 64)
    chan = x_ref.shape[0]
    for color in range(colors):
        below = lax.rem(tile + color, 2) == 0
        parts = []
        for p in range(2):
            last = x_ref[:, (p + 1) * half - 2 * span : (p + 1) * half]
            first = x_ref[:, p * half : p * half + 2 * span]
            parts += [jnp.where(below, last, first), jnp.zeros((chan, seg - 2 * span), bf16)]
        outs[color][...] = jnp.concatenate(parts, axis=1)


def selection(rows, per_col, width, cols, span, dest, tokens):
    r = lax.broadcasted_iota(jnp.int32, (rows, 1), 0)
    w = jnp.zeros_like(r)
    for k in range(1, width):
        w = w + (r >= k * per_col).astype(jnp.int32)
    h = r - w * per_col
    col = dest * cols - 2 + w
    good = (col >= 0) & (col < span) & (r < width * per_col)
    token = jnp.where(good, h * span + col, -1)
    lane = lax.broadcasted_iota(jnp.int32, (rows, tokens), 1)
    return jnp.where(lane == token, 1.0, 0.0).astype(bf16)


def pack_kernel(count, cols, x_ref, *outs):
    seq = lax.axis_index("seq")
    width, span = cols + 4, count * cols
    half = ROWS_DEV * span
    parts = [x_ref[:, p * half : (p + 1) * half] for p in range(2)]
    for d in range(count):
        dest = lax.rem(seq + d, count)
        pick = selection(width * ROWS_DEV, ROWS_DEV, width, cols, span, dest, half)
        both = jnp.concatenate([dot_nt(pick, part) for part in parts], axis=1)
        outs[d][0 : width * ROWS_DEV, :] = both.astype(bf16)


def border_kernel(count, cols, colors, *refs):
    edges = refs[:colors]
    outs = refs[colors + count : colors + 2 * count]
    held, sems = refs[colors + 2 * count :]
    seq = lax.axis_index("seq")
    width, span = cols + 4, count * cols
    rows = border_rows(width)
    seg = round_up(2 * span, 64)
    copies = []
    for d in range(count):
        dest = lax.rem(seq + d, count)
        pick = selection(rows, 2, width, cols, span, dest, seg)
        for color in range(colors):
            x = edges[color][...]
            both = jnp.concatenate([dot_nt(pick, x[:, p * seg : (p + 1) * seg]) for p in range(2)], axis=1)
            held[d, color * rows : (color + 1) * rows, :] = both.astype(bf16)
        to = outs[d].at[pl.ds(width * ROWS_DEV, colors * rows)]
        copies.append(pltpu.make_async_copy(held.at[d], to, sems.at[d]))
        copies[-1].start()
    for copy in copies:
        copy.wait()


def conv_kernel(cfg, *refs):
    width, kinds, ring, d = cfg
    extra = {2: 2, 3: 2}.get(d, 0)
    own_ref, other_ref, gain_ref, w_ref, bias_ref = refs[:5]
    before = refs[5 : 5 + extra]
    rest = refs[5 + extra :]
    pad_ref, raw_ref, lhs_ref = rest[-3:]
    rest = rest[:-3]
    part_ref = rest[0]
    mid_ref = {2: rest[-1], 3: rest[0]}.get(d)
    if d == 3:
        mid_ref, part_ref = rest
    tile, chan_id, tiles = lax.axis_index("tile"), lax.axis_index("chan"), lax.axis_size("tile")
    seq, seqs = lax.axis_index("seq"), lax.axis_size("seq")
    chan = gain_ref.shape[1] // 2
    out_rows = (width - 2) * PITCH
    gain = gain_ref[...]
    pad_ref[...] = jnp.zeros_like(pad_ref)
    raw_ref[...] = jnp.zeros_like(raw_ref)
    main = width * ROWS_DEV

    def place(raw, act, top):
        first = HEAD - 2 if top else HEAD + ROWS_DEV
        for w in range(width):
            pad_ref[w * PITCH + first : w * PITCH + first + 2, :] = act[2 * w : 2 * w + 2]
            raw_ref[w * PITCH + first : w * PITCH + first + 2, :] = raw[2 * w : 2 * w + 2]

    fields = []
    for p in range(2):
        mine = own_ref[:, p * chan : (p + 1) * chan]
        theirs = other_ref[:, p * chan : (p + 1) * chan]
        low = jnp.where(chan_id == 0, mine, theirs)
        high = jnp.where(chan_id == 0, theirs, mine)
        x = jnp.concatenate([low, high], axis=1).astype(f32)
        scale = lax.rsqrt(jnp.mean(x * x, axis=-1, keepdims=True) + norm_eps)
        v = x * scale * gain
        act = v / (1.0 + jnp.exp(-v))
        raw = mine.astype(f32)
        for w in range(width):
            to = slice(w * PITCH + HEAD, w * PITCH + HEAD + ROWS_DEV)
            pad_ref[to, :] = act[w * ROWS_DEV : (w + 1) * ROWS_DEV]
            raw_ref[to, :] = raw[w * ROWS_DEV : (w + 1) * ROWS_DEV]
        for k, kind in enumerate(kinds):
            at = main + k * border_rows(width)
            raw_k, act_k = raw[at : at + 2 * width], act[at : at + 2 * width]
            if kind in ("top", "bottom"):
                place(raw_k, act_k, kind == "top")
            else:
                below = lax.rem(tile + int(kind), 2) == 0
                pl.when(below)(functools.partial(place, raw_k, act_k, False))
                pl.when(jnp.logical_not(below))(functools.partial(place, raw_k, act_k, True))
        for dh in range(3):
            shifted = pad_ref[HEAD - 2 + dh : HEAD - 2 + dh + width * PITCH, :]
            lhs_ref[p, :, dh * 2 * chan : (dh + 1) * 2 * chan] = shifted.astype(bf16)
        part_ref[p] = raw_ref[PITCH + HEAD - 1 : PITCH + HEAD - 1 + out_rows, :]

    lhs = jnp.concatenate(
        [lhs_ref[:, dw * PITCH : dw * PITCH + out_rows, :].reshape(2 * out_rows, 6 * chan) for dw in range(3)], axis=1
    )
    zero = jnp.zeros((out_rows, chan), f32)
    for dt in (2, 1, 0):
        taps = [w_ref[dt * 9 + dh * 3 + dw] for dw in range(3) for dh in range(3)]
        total = dot_nt(lhs, jnp.concatenate(taps, axis=1)).reshape(2, out_rows, chan)
        if dt == 2:
            part_ref[0] += total[0]
            part_ref[1] += total[1]
        elif dt == 1:
            part_ref[1] += total[0]
            part_ref[2] = total[1]
        else:
            part_ref[2] += total[0]
            part_ref[3] = total[1]

    if d >= 2:
        r = lax.broadcasted_iota(jnp.int32, (out_rows, 1), 0)
        h = jnp.bitwise_and(r, PITCH - 1) - 1
        good = (h >= jnp.where(tile == 0, 0, -1)) & (h < jnp.where(tile == tiles - 1, ROWS_DEV, ROWS_DEV + 1))
        good = good & (r >= jnp.where(seq == 0, PITCH, 0)) & (r < jnp.where(seq == seqs - 1, out_rows - PITCH, out_rows))
        base = seq if ring else 0
        if d == 2:
            sums = [(0, before[0], before[1]), (1, before[1], part_ref)]
        else:
            sums = [(2, before[1], part_ref), (3, part_ref, before[0])]
        for k, (shift, now, past) in enumerate(sums):
            first = lax.rem(base - shift + PAIRS, PAIRS) == 0
            mids = []
            for p in range(2):
                value = now[p] + jnp.where(first, 0.0, past[2 + p]) + bias_ref[...]
                mids.append(jnp.where(good, value, 0.0))
            mid_ref[k] = jnp.concatenate(mids, axis=1).astype(bf16)


def tap_kernel(w_ref, out_ref, rows_ref):
    out_chan, chans = w_ref.shape[1:]
    rows_ref[...] = jnp.zeros_like(rows_ref)
    taps = [[w_ref[dr * 3 + ds].astype(f32) for ds in range(3)] for dr in range(3)]
    by_row = [[[taps[0][s] for s in range(3)], [taps[1][s] + taps[2][s] for s in range(3)]]]
    by_row.append([[taps[0][s] + taps[1][s] for s in range(3)], [taps[2][s] for s in range(3)]])
    for i in range(2):
        for dw in range(3):
            for a in range(2):
                t = by_row[i][a]
                zero = jnp.zeros_like(t[0])
                left = (t[0], t[1] + t[2], zero)[dw]
                right = (zero, t[0] + t[1], t[2])[dw]
                for k in range(chans // 128):
                    lanes = slice(k * 128, (k + 1) * 128)
                    rows_ref[pl.ds(0, out_chan, stride=2), :] = left[:, lanes]
                    rows_ref[pl.ds(1, out_chan, stride=2), :] = right[:, lanes]
                    to = a * chans + k * 128
                    out_ref[i, dw, :, to : to + 128] = rows_ref[...].astype(bf16)


def up_kernel(cfg, *refs):
    mid_w, ring, first = cfg
    own_ref, other_ref, w_ref, bias_ref = refs[:4]
    out_ref, lhs_ref, rows_ref, held_ref, sems = refs[-5:]
    chan_id = lax.axis_index("chan")
    base = lax.axis_index("seq") if ring else 0
    chan = own_ref.shape[2] // 2
    cols = mid_w - 2
    keep = (mid_w - 1) * PITCH + ROWS_DEV
    count = own_ref.shape[0]
    frames = 2 * count
    lanes = w_ref.shape[2]
    span = cols * PITCH
    lhs_ref[:, keep:, :] = jnp.zeros_like(lhs_ref[:, keep:, :])
    for k in range(count):
        for p in range(2):
            mine = own_ref[k, :, p * chan : (p + 1) * chan]
            theirs = other_ref[k, :, p * chan : (p + 1) * chan]
            low = jnp.where(chan_id == 0, mine, theirs)
            high = jnp.where(chan_id == 0, theirs, mine)
            x = jnp.concatenate([low, high], axis=1).astype(f32)
            for a in range(3):
                lhs_ref[2 * k + p, 0:keep, a * 2 * chan : (a + 1) * 2 * chan] = x[a : a + keep].astype(bf16)
    for i in range(2):
        lhs = jnp.concatenate(
            [
                lhs_ref[:, dw * PITCH : dw * PITCH + span, i * 2 * chan : (i + 2) * 2 * chan].reshape(frames * span, 4 * chan)
                for dw in range(3)
            ],
            axis=1,
        )
        total = dot_nt(lhs, jnp.concatenate([w_ref[i, dw] for dw in range(3)], axis=1))
        total = total.reshape(frames, span, lanes)
        for f in range(frames):
            for w in range(cols):
                for k in range(lanes // 128):
                    piece = total[f, w * PITCH : w * PITCH + ROWS_DEV, k * 128 : (k + 1) * 128]
                    rows_ref[k, f * cols + w, pl.ds(i, ROWS_DEV, stride=2), :] = piece
    bias = bias_ref[...]
    copies = []
    for k in range(count):
        for f in (2 * k, 2 * k + 1):
            for w in range(cols):
                row = jnp.concatenate([rows_ref[c, f * cols + w] for c in range(lanes // 128)], axis=1)
                held_ref[f, w] = (row[:, : held_ref.shape[3]] + bias).astype(bf16)
        frame = 2 * lax.rem(base - (first + k) + PAIRS, PAIRS)
        copies.append(pltpu.make_async_copy(held_ref.at[pl.ds(2 * k, 2)], out_ref.at[pl.ds(frame, 2)], sems.at[k]))
        copies[-1].start()
    for copy in copies:
        copy.wait()


def swap_chan(x):
    return lax.ppermute(x, "chan", [(0, 1), (1, 0)])


def tile_pairs(color, tiles):
    out = []
    for t in range(color, tiles - 1, 2):
        out += [(t, t + 1), (t + 1, t)]
    return out


def arrive_by_ring(latents, cols):
    seqs, tiles = lax.axis_size("seq"), lax.axis_size("tile")
    colors = min(2, tiles - 1)
    width, span = cols + 4, cols * seqs
    chan = latents.shape[2]
    x = latents[0].T
    edge = jax.ShapeDtypeStruct((chan, 2 * round_up(2 * span, 64)), bf16)
    edges = call(functools.partial(edge_kernel, span, colors), [edge] * colors, [VM], [VM] * colors, [], 4, "edge")(x)
    edges = [lax.ppermute(e, "tile", tile_pairs(color, tiles)) for color, e in enumerate(edges)]
    border = border_rows(width)
    rows = width * ROWS_DEV + colors * border
    block = jax.ShapeDtypeStruct((rows, 2 * chan), bf16)
    windows = call(functools.partial(pack_kernel, seqs, cols), [block] * seqs, [VM], [VM] * seqs, [], 12, "pack", flops=2 * 10**9)(x)
    windows = call(
        functools.partial(border_kernel, seqs, cols, colors),
        [block] * seqs,
        [VM] * colors + [ANY] * seqs,
        [ANY] * seqs,
        [pltpu.VMEM((seqs, colors * border, 2 * chan), bf16), pltpu.SemaphoreType.DMA((seqs,))],
        4,
        "border",
        aliases={colors + d: d for d in range(seqs)},
    )(*edges, *windows)
    blocks = [windows[0]]
    for d in range(1, seqs):
        blocks.append(lax.ppermute(windows[d], "seq", [(i, (i + d) % seqs) for i in range(seqs)]))
    return blocks, [str(c) for c in range(colors)]


def extended(cells, sides, width):
    for axis, dim in sides:
        count = lax.axis_size(axis)
        ends = count - 1
        head = lax.slice_in_dim(cells, 0, width, axis=dim)
        tail = lax.slice_in_dim(cells, cells.shape[dim] - width, cells.shape[dim], axis=dim)
        cells = jnp.concatenate(
            [
                lax.ppermute(tail, axis, [(i, (i + 1) % count) for i in range(ends)]),
                cells,
                lax.ppermute(head, axis, [((i + 1) % count, i) for i in range(ends)]),
            ],
            axis=dim,
        )
    return cells


def arrive_by_all_to_all(latents, cols):
    seqs = lax.axis_size("seq")
    chan = latents.shape[2]
    width = cols + 4
    arranged = latents[0].reshape(FRAMES * ROWS_DEV // seqs, seqs, cols, chan)
    regrouped = lax.all_to_all(arranged, "seq", split_axis=1, concat_axis=0, tiled=True)
    field = regrouped.reshape(FRAMES, ROWS_DEV, cols, chan)
    field = extended(field, (("seq", 2), ("tile", 1)), 2)
    paired = field.reshape(PAIRS, 2, ROWS_DEV + 4, width, chan).transpose(0, 3, 2, 1, 4)
    paired = paired.reshape(PAIRS, width, ROWS_DEV + 4, 2 * chan)
    spare = ((0, border_rows(width) - 2 * width), (0, 0))
    blocks = []
    for d in range(PAIRS):
        k = -d % PAIRS
        pieces = [paired[k, :, 2:-2].reshape(-1, 2 * chan)]
        pieces += [jnp.pad(b.reshape(-1, 2 * chan), spare) for b in (paired[k, :, :2], paired[k, :, -2:])]
        blocks.append(jnp.concatenate(pieces, axis=0))
    return blocks, ["top", "bottom"]


def body(latents, norm_gain, conv_weight, conv_bias, upsample_weight, upsample_bias):
    chan, out_chan = conv_bias.shape[0], upsample_bias.shape[0]
    cols = latents.shape[1] // (FRAMES * ROWS_DEV)
    width, mid_w = cols + 4, cols + 2
    out_rows = mid_w * PITCH
    ring = 2 * lax.axis_size("seq") == FRAMES
    blocks, kinds = arrive_by_ring(latents, cols) if ring else arrive_by_all_to_all(latents, cols)

    up_lanes = round_up(2 * out_chan, 128)
    taps = upsample_weight.transpose(0, 1, 3, 2).reshape(9, out_chan, 2 * chan)
    up_weights = call(
        tap_kernel,
        jax.ShapeDtypeStruct((2, 3, up_lanes, 4 * chan), bf16),
        [VM],
        VM,
        [pltpu.VMEM((up_lanes, 128), f32)],
        12,
        "taps",
        flops=10**9,
    )(taps)
    up_bias = jnp.repeat(upsample_bias, 2)[None]

    weights = conv_weight.transpose(0, 1, 2, 4, 3).reshape(27, chan, 2 * chan)
    gain, bias = norm_gain[None], conv_bias[None]
    part = jax.ShapeDtypeStruct((4, out_rows, chan), f32)
    mid = jax.ShapeDtypeStruct((2, out_rows, 2 * chan), bf16)
    work = [
        pltpu.VMEM((width * PITCH + 2 * HEAD, 2 * chan), f32),
        pltpu.VMEM((width * PITCH + 2 * HEAD, chan), f32),
        pltpu.VMEM((2, width * PITCH, 6 * chan), bf16),
    ]

    def conv(d, out_shape, *before, scratch=()):
        return call(
            functools.partial(conv_kernel, (width, kinds, ring, d)),
            out_shape,
            [VM] * (5 + len(before)),
            [VM] * len(out_shape),
            [*scratch, *work],
            14,
            f"conv{d}",
            flops=2 * 2 * out_rows * 27 * 2 * chan * 256,
        )(blocks[d], swap_chan(blocks[d]), gain, weights, bias, *before)

    def upsample(mids, first, out=None):
        held = () if out is None else (out,)
        return call(
            functools.partial(up_kernel, (mid_w, ring, first)),
            jax.ShapeDtypeStruct((FRAMES, cols, 2 * ROWS_DEV, 2 * out_chan), bf16),
            [VM] * 4 + [ANY] * len(held),
            ANY,
            [
                pltpu.VMEM((4, out_rows, 6 * chan), bf16),
                pltpu.VMEM((up_lanes // 128, 4 * cols, 2 * ROWS_DEV, 128), f32),
                pltpu.VMEM((4, cols, 2 * ROWS_DEV, 2 * out_chan), bf16),
                pltpu.SemaphoreType.DMA((2,)),
            ],
            14,
            f"up{first}",
            flops=2 * 2 * 4 * cols * PITCH * 12 * chan * 256,
            aliases={4: 0} if held else None,
        )(mids, swap_chan(mids), up_weights, up_bias, *held)

    (part0,) = conv(0, [part])
    (part1,) = conv(1, [part])
    part2, early = conv(2, [part, mid], part0, part1)
    decoded = upsample(early, 0)
    (late,) = conv(3, [mid], part0, part2, scratch=[pltpu.VMEM((4, out_rows, chan), f32)])
    decoded = upsample(late, 2, decoded)
    return decoded.transpose(0, 2, 1, 3)


def solution(mesh):
    in_specs = (
        P("tile", ("groups", "seq"), "chan"),
        P(),
        P(None, None, None, None, "chan"),
        P("chan"),
        P(None, None, None, "chan"),
        P("chan"),
    )
    out_specs = P(None, ("groups", "tile"), "seq", "chan")
    return jax.shard_map(body, mesh=mesh, in_specs=in_specs, out_specs=out_specs, check_vma=False)
```

```python
import functools

import jax
import jax.numpy as jnp
from jax import lax
from jax.experimental import pallas as pl
from jax.experimental.pallas import tpu as pltpu
from jax.sharding import PartitionSpec as P


FRAMES = 8
ROWS_DEV = 24
PAIRS = FRAMES // 2
ORDER = (0, 1, 3, 2)
PITCH = 32
HEAD = 8

norm_eps = 1e-06
f32 = jnp.float32
bf16 = jnp.bfloat16
VM = pl.BlockSpec(memory_space=pltpu.VMEM)
ANY = pl.BlockSpec(memory_space=pl.ANY)
MIB = 1024 * 1024


def dot_nt(a, b):
    return lax.dot_general(a, b, (((1,), (1,)), ((), ())), preferred_element_type=f32)


def call(kernel, out_shape, in_specs, out_specs, scratch, limit, flops=0, moved=0, aliases=None):
    return pl.pallas_call(
        kernel,
        out_shape=out_shape,
        in_specs=in_specs,
        out_specs=out_specs,
        scratch_shapes=list(scratch),
        compiler_params=pltpu.CompilerParams(vmem_limit_bytes=limit * MIB),
        input_output_aliases=aliases or {},
        cost_estimate=pl.CostEstimate(flops=flops, bytes_accessed=moved, transcendentals=0),
    )


def round_up(n, k):
    return -(-n // k) * k


def border_rows(width):
    return round_up(2 * width, 8)


def selection(rows, per_col, width, cols, span, dest, tokens):
    r = lax.broadcasted_iota(jnp.int32, (rows, 1), 0)
    w = jnp.zeros_like(r)
    for k in range(1, width):
        w = w + (r >= k * per_col).astype(jnp.int32)
    h = r - w * per_col
    col = dest * cols - 2 + w
    good = (col >= 0) & (col < span) & (r < width * per_col)
    token = jnp.where(good, h * span + col, -1)
    lane = lax.broadcasted_iota(jnp.int32, (rows, tokens), 1)
    return jnp.where(lane == token, 1.0, 0.0).astype(bf16)


def pack_kernel(count, cols, colors, x_ref, *outs):
    seq, tile = lax.axis_index("seq"), lax.axis_index("tile")
    width, span = cols + 4, count * cols
    half = ROWS_DEV * span
    seg = round_up(2 * span, 64)
    chan = x_ref.shape[0]
    rows = width * ROWS_DEV
    for color in range(colors):
        below = lax.rem(tile + color, 2) == 0
        parts = []
        for p in range(2):
            last = x_ref[:, (p + 1) * half - 2 * span : (p + 1) * half]
            first = x_ref[:, p * half : p * half + 2 * span]
            parts += [jnp.where(below, last, first), jnp.zeros((chan, seg - 2 * span), bf16)]
        outs[color][...] = jnp.concatenate(parts, axis=1)
    for d in range(count):
        pick = selection(rows, ROWS_DEV, width, cols, span, lax.rem(seq + d, count), half)
        both = jnp.concatenate([dot_nt(pick, x_ref[:, p * half : (p + 1) * half]) for p in range(2)], axis=1)
        outs[colors + d][0:rows, :] = both.astype(bf16)


def border_kernel(count, cols, colors, *refs):
    edges = refs[:colors]
    outs = refs[colors + count : colors + 2 * count]
    held, sems = refs[colors + 2 * count :]
    seq = lax.axis_index("seq")
    width, span = cols + 4, count * cols
    rows = border_rows(width)
    seg = round_up(2 * span, 64)
    picks = [selection(rows, 2, width, cols, span, lax.rem(seq + d, count), seg) for d in range(count)]
    pick = jnp.concatenate(picks, axis=0)
    for color in range(colors):
        x = edges[color][...]
        both = jnp.concatenate([dot_nt(pick, x[:, p * seg : (p + 1) * seg]) for p in range(2)], axis=1)
        for d in range(count):
            held[d, color * rows : (color + 1) * rows, :] = both[d * rows : (d + 1) * rows].astype(bf16)
    copies = []
    for d in range(count):
        to = outs[d].at[pl.ds(width * ROWS_DEV, colors * rows)]
        copies.append(pltpu.make_async_copy(held.at[d], to, sems.at[d]))
        copies[-1].start()
    for copy in copies:
        copy.wait()


def conv_kernel(cfg, *refs):
    width, kinds, ring, d, done = cfg
    own_ref, other_ref, gain_ref, w_ref, bias_ref = refs[:5]
    others = sorted({k for now, past in done for k in (now, past)} - {d})
    parts = dict(zip(others, refs[5:]))
    rest = refs[5 + len(others) :]
    pad_ref, raw_ref, lhs_ref = rest[-3:]
    mid_ref = rest[0] if done else None
    part_ref = rest[1] if done else rest[0]
    parts[d] = part_ref
    tile, chan_id, tiles = lax.axis_index("tile"), lax.axis_index("chan"), lax.axis_size("tile")
    seq, seqs = lax.axis_index("seq"), lax.axis_size("seq")
    chan = gain_ref.shape[0] // 2
    out_rows = (width - 2) * PITCH
    gain = gain_ref[...].reshape(1, 2 * chan)
    pad_ref[...] = jnp.zeros_like(pad_ref)
    raw_ref[...] = jnp.zeros_like(raw_ref)
    main = width * ROWS_DEV

    def place(raw, act, first):
        for w in range(width):
            to = slice(w * PITCH + first, w * PITCH + first + 2)
            pad_ref[to, :] = act[2 * w : 2 * w + 2]
            raw_ref[to, :] = raw[2 * w : 2 * w + 2]

    for p in range(2):
        mine = own_ref[:, p * chan : (p + 1) * chan]
        theirs = other_ref[:, p * chan : (p + 1) * chan]
        low = jnp.where(chan_id == 0, mine, theirs)
        high = jnp.where(chan_id == 0, theirs, mine)
        x = jnp.concatenate([low, high], axis=1).astype(f32)
        scale = lax.rsqrt(jnp.mean(x * x, axis=-1, keepdims=True) + norm_eps)
        v = x * scale * gain
        act = v / (1.0 + jnp.exp(-v))
        raw = mine.astype(f32)
        for w in range(width):
            to = slice(w * PITCH + HEAD, w * PITCH + HEAD + ROWS_DEV)
            pad_ref[to, :] = act[w * ROWS_DEV : (w + 1) * ROWS_DEV]
            raw_ref[to, :] = raw[w * ROWS_DEV : (w + 1) * ROWS_DEV]
        tops, bottoms = [], []
        for k, kind in enumerate(kinds):
            at = main + k * border_rows(width)
            pieces = raw[at : at + 2 * width], act[at : at + 2 * width]
            if kind == "top":
                tops.append(pieces)
            elif kind == "bottom":
                bottoms.append(pieces)
            else:
                below = lax.rem(tile + int(kind), 2) == 0
                tops.append([jnp.where(below, 0.0, piece) for piece in pieces])
                bottoms.append([jnp.where(below, piece, 0.0) for piece in pieces])
        for found, first in ((tops, HEAD - 2), (bottoms, HEAD + ROWS_DEV)):
            if found:
                place(functools.reduce(jnp.add, [f[0] for f in found]), functools.reduce(jnp.add, [f[1] for f in found]), first)
        for dh in range(3):
            shifted = pad_ref[HEAD - 2 + dh : HEAD - 2 + dh + width * PITCH, :]
            lhs_ref[p, :, dh * 2 * chan : (dh + 1) * 2 * chan] = shifted.astype(bf16)
        part_ref[p] = raw_ref[PITCH + HEAD - 1 : PITCH + HEAD - 1 + out_rows, :]

    lhs = jnp.concatenate(
        [lhs_ref[:, dw * PITCH : dw * PITCH + out_rows, :].reshape(2 * out_rows, 6 * chan) for dw in range(3)], axis=1
    )
    zero = jnp.zeros((out_rows, chan), f32)
    for dt in (2, 1, 0):
        taps = [w_ref[dt * 9 + dh * 3 + dw] for dw in range(3) for dh in range(3)]
        total = dot_nt(lhs, jnp.concatenate(taps, axis=1)).reshape(2, out_rows, chan)
        if dt == 2:
            part_ref[0] += total[0]
            part_ref[1] += total[1]
        elif dt == 1:
            part_ref[1] += total[0]
            part_ref[2] = total[1]
        else:
            part_ref[2] += total[0]
            part_ref[3] = total[1]

    if done:
        r = lax.broadcasted_iota(jnp.int32, (out_rows, 1), 0)
        h = jnp.bitwise_and(r, PITCH - 1) - 1
        good = (h >= jnp.where(tile == 0, 0, -1)) & (h < jnp.where(tile == tiles - 1, ROWS_DEV, ROWS_DEV + 1))
        good = good & (r >= jnp.where(seq == 0, PITCH, 0)) & (r < jnp.where(seq == seqs - 1, out_rows - PITCH, out_rows))
        base = seq if ring else 0
        for k, (now, past) in enumerate(done):
            first = lax.rem(base - now + PAIRS, PAIRS) == 0
            mids = []
            for p in range(2):
                value = parts[now][p] + jnp.where(first, 0.0, parts[past][2 + p]) + bias_ref[...]
                mids.append(jnp.where(good, value, 0.0))
            mid_ref[k] = jnp.concatenate(mids, axis=1).astype(bf16)


def tap_kernel(w_ref, bias_ref, out_ref, wide_ref, rows_ref):
    out_chan, chans = w_ref.shape[1:]
    lane = lax.broadcasted_iota(jnp.int32, (out_chan, wide_ref.shape[1]), 1)
    row = lax.broadcasted_iota(jnp.int32, lane.shape, 0)
    spread = jnp.where((lane == 2 * row) | (lane == 2 * row + 1), 1.0, 0.0)
    dims = (((1,), (0,)), ((), ()))
    wide_ref[...] = lax.dot_general(bias_ref[...], spread, dims, precision=lax.Precision.HIGHEST, preferred_element_type=f32)
    rows_ref[...] = jnp.zeros_like(rows_ref)
    taps = [[w_ref[dr * 3 + ds].astype(f32) for ds in range(3)] for dr in range(3)]
    by_row = [[[taps[0][s] for s in range(3)], [taps[1][s] + taps[2][s] for s in range(3)]]]
    by_row.append([[taps[0][s] + taps[1][s] for s in range(3)], [taps[2][s] for s in range(3)]])
    for i in range(2):
        for dw in range(3):
            for a in range(2):
                t = by_row[i][a]
                zero = jnp.zeros_like(t[0])
                left = (t[0], t[1] + t[2], zero)[dw]
                right = (zero, t[0] + t[1], t[2])[dw]
                for k in range(chans // 128):
                    lanes = slice(k * 128, (k + 1) * 128)
                    rows_ref[pl.ds(0, out_chan, stride=2), :] = left[:, lanes]
                    rows_ref[pl.ds(1, out_chan, stride=2), :] = right[:, lanes]
                    to = a * chans + k * 128
                    out_ref[i, dw, :, to : to + 128] = rows_ref[...].astype(bf16)


def up_kernel(cfg, *refs):
    mid_w, ring, shifts = cfg
    own_ref, other_ref, w_ref, bias_ref = refs[:4]
    out_ref, lhs_ref, rows_ref, held_ref, sems = refs[-5:]
    chan_id = lax.axis_index("chan")
    base = lax.axis_index("seq") if ring else 0
    chan = own_ref.shape[2] // 2
    cols = mid_w - 2
    keep = (mid_w - 1) * PITCH + ROWS_DEV
    count = own_ref.shape[0]
    frames = 2 * count
    lanes = w_ref.shape[2]
    span = cols * PITCH
    lhs_ref[:, keep:, :] = jnp.zeros_like(lhs_ref[:, keep:, :])
    for k in range(count):
        for p in range(2):
            mine = own_ref[k, :, p * chan : (p + 1) * chan]
            theirs = other_ref[k, :, p * chan : (p + 1) * chan]
            low = jnp.where(chan_id == 0, mine, theirs)
            high = jnp.where(chan_id == 0, theirs, mine)
            x = jnp.concatenate([low, high], axis=1).astype(f32)
            for a in range(3):
                lhs_ref[2 * k + p, 0:keep, a * 2 * chan : (a + 1) * 2 * chan] = x[a : a + keep].astype(bf16)
    for i in range(2):
        lhs = jnp.concatenate(
            [
                lhs_ref[:, dw * PITCH : dw * PITCH + span, i * 2 * chan : (i + 2) * 2 * chan].reshape(frames * span, 4 * chan)
                for dw in range(3)
            ],
            axis=1,
        )
        total = dot_nt(lhs, jnp.concatenate([w_ref[i, dw] for dw in range(3)], axis=1))
        total = total.reshape(frames, span, lanes)
        for f in range(frames):
            for w in range(cols):
                for k in range(lanes // 128):
                    piece = total[f, w * PITCH : w * PITCH + ROWS_DEV, k * 128 : (k + 1) * 128]
                    rows_ref[k, f * cols + w, pl.ds(i, ROWS_DEV, stride=2), :] = piece
    bias = bias_ref[:, : held_ref.shape[3]]
    copies = []
    for k in range(count):
        for f in (2 * k, 2 * k + 1):
            for w in range(cols):
                row = jnp.concatenate([rows_ref[c, f * cols + w] for c in range(lanes // 128)], axis=1)
                held_ref[f, w] = (row[:, : held_ref.shape[3]] + bias).astype(bf16)
        frame = 2 * lax.rem(base - shifts[k] + PAIRS, PAIRS)
        copies.append(pltpu.make_async_copy(held_ref.at[pl.ds(2 * k, 2)], out_ref.at[pl.ds(frame, 2)], sems.at[k]))
        copies[-1].start()
    for copy in copies:
        copy.wait()


def swap_chan(x):
    return lax.ppermute(x, "chan", [(0, 1), (1, 0)])


def tile_pairs(color, tiles):
    out = []
    for t in range(color, tiles - 1, 2):
        out += [(t, t + 1), (t + 1, t)]
    return out


def arrive_by_ring(latents, cols):
    seqs, tiles = lax.axis_size("seq"), lax.axis_size("tile")
    colors = min(2, tiles - 1)
    width, span = cols + 4, cols * seqs
    chan = latents.shape[2]
    x = latents[0].T
    border = border_rows(width)
    rows = width * ROWS_DEV + colors * border
    edge = jax.ShapeDtypeStruct((chan, 2 * round_up(2 * span, 64)), bf16)
    block = jax.ShapeDtypeStruct((rows, 2 * chan), bf16)
    packed = call(
        functools.partial(pack_kernel, seqs, cols, colors),
        [edge] * colors + [block] * seqs,
        [VM],
        [VM] * (colors + seqs),
        [],
        12,
        flops=2 * 10**9,
    )(x)
    edges, windows = packed[:colors], packed[colors:]
    edges = [lax.ppermute(e, "tile", tile_pairs(color, tiles)) for color, e in enumerate(edges)]
    windows = call(
        functools.partial(border_kernel, seqs, cols, colors),
        [block] * seqs,
        [VM] * colors + [ANY] * seqs,
        [ANY] * seqs,
        [pltpu.VMEM((seqs, colors * border, 2 * chan), bf16), pltpu.SemaphoreType.DMA((seqs,))],
        4,
        aliases={colors + d: d for d in range(seqs)},
    )(*edges, *windows)
    blocks = [windows[0]]
    for d in range(1, seqs):
        blocks.append(lax.ppermute(windows[d], "seq", [(i, (i + d) % seqs) for i in range(seqs)]))
    return blocks, [str(c) for c in range(colors)]


def extended(cells, sides, width):
    for axis, dim in sides:
        count = lax.axis_size(axis)
        ends = count - 1
        head = lax.slice_in_dim(cells, 0, width, axis=dim)
        tail = lax.slice_in_dim(cells, cells.shape[dim] - width, cells.shape[dim], axis=dim)
        cells = jnp.concatenate(
            [
                lax.ppermute(tail, axis, [(i, (i + 1) % count) for i in range(ends)]),
                cells,
                lax.ppermute(head, axis, [((i + 1) % count, i) for i in range(ends)]),
            ],
            axis=dim,
        )
    return cells


def arrive_by_all_to_all(latents, cols):
    seqs = lax.axis_size("seq")
    chan = latents.shape[2]
    width = cols + 4
    arranged = latents[0].reshape(FRAMES * ROWS_DEV // seqs, seqs, cols, chan)
    regrouped = lax.all_to_all(arranged, "seq", split_axis=1, concat_axis=0, tiled=True)
    field = regrouped.reshape(FRAMES, ROWS_DEV, cols, chan)
    field = extended(field, (("seq", 2), ("tile", 1)), 2)
    paired = field.reshape(PAIRS, 2, ROWS_DEV + 4, width, chan).transpose(0, 3, 2, 1, 4)
    paired = paired.reshape(PAIRS, width, ROWS_DEV + 4, 2 * chan)
    spare = ((0, border_rows(width) - 2 * width), (0, 0))
    blocks = []
    for d in range(PAIRS):
        k = -d % PAIRS
        pieces = [paired[k, :, 2:-2].reshape(-1, 2 * chan)]
        pieces += [jnp.pad(b.reshape(-1, 2 * chan), spare) for b in (paired[k, :, :2], paired[k, :, -2:])]
        blocks.append(jnp.concatenate(pieces, axis=0))
    return blocks, ["top", "bottom"]


def block_body(latents, norm_gain, conv_weight, conv_bias, upsample_weight, upsample_bias):
    chan, out_chan = conv_bias.shape[0], upsample_bias.shape[0]
    cols = latents.shape[1] // (FRAMES * ROWS_DEV)
    width, mid_w = cols + 4, cols + 2
    out_rows = mid_w * PITCH
    ring = 2 * lax.axis_size("seq") == FRAMES
    blocks, kinds = arrive_by_ring(latents, cols) if ring else arrive_by_all_to_all(latents, cols)

    up_lanes = round_up(2 * out_chan, 128)
    taps = upsample_weight.transpose(0, 1, 3, 2).reshape(9, out_chan, 2 * chan)
    up_weights, up_bias = call(
        tap_kernel,
        [jax.ShapeDtypeStruct((2, 3, up_lanes, 4 * chan), bf16), jax.ShapeDtypeStruct((1, up_lanes), f32)],
        [VM, VM],
        [VM, VM],
        [pltpu.VMEM((up_lanes, 128), f32)],
        12,
        flops=10**9,
    )(taps, upsample_bias[None])

    weights = conv_weight.transpose(0, 1, 2, 4, 3).reshape(27, chan, 2 * chan)
    gain, bias = norm_gain, conv_bias[None]
    part = jax.ShapeDtypeStruct((4, out_rows, chan), f32)
    work = [
        pltpu.VMEM((width * PITCH + 2 * HEAD, 2 * chan), f32),
        pltpu.VMEM((width * PITCH + 2 * HEAD, chan), f32),
        pltpu.VMEM((2, width * PITCH, 6 * chan), bf16),
    ]

    def conv(d, parts=None, done=()):
        keep = d != ORDER[-1]
        others = sorted({k for pair in done for k in pair} - {d})
        before = [parts[k] for k in others]
        outs = [jax.ShapeDtypeStruct((len(done), out_rows, 2 * chan), bf16)] if done else []
        outs += [part] if keep else []
        other = swap_chan(blocks[d])
        return call(
            functools.partial(conv_kernel, (width, kinds, ring, d, done)),
            outs,
            [VM] * (5 + len(before)),
            [VM] * len(outs),
            ([] if keep else [pltpu.VMEM((4, out_rows, chan), f32)]) + work,
            14,
            flops=2 * 2 * out_rows * 27 * 2 * chan * 256,
        )(blocks[d], other, gain, weights, bias, *before)

    def upsample(mids, shifts, out=None):
        held = () if out is None else (out,)
        count = len(shifts)
        other = swap_chan(mids)
        return call(
            functools.partial(up_kernel, (mid_w, ring, shifts)),
            jax.ShapeDtypeStruct((FRAMES, cols, 2 * ROWS_DEV, 2 * out_chan), bf16),
            [VM] * 4 + [ANY] * len(held),
            ANY,
            [
                pltpu.VMEM((2 * count, out_rows, 6 * chan), bf16),
                pltpu.VMEM((up_lanes // 128, 2 * count * cols, 2 * ROWS_DEV, 128), f32),
                pltpu.VMEM((2 * count, cols, 2 * ROWS_DEV, 2 * out_chan), bf16),
                pltpu.SemaphoreType.DMA((count,)),
            ],
            14,
            flops=2 * 2 * 2 * count * cols * PITCH * 12 * chan * 256,
            aliases={4: 0} if held else None,
        )(mids, other, up_weights, up_bias, *held)

    parts = {}
    (parts[0],) = conv(0)
    mid0, parts[1] = conv(1, parts, ((0, 1),))
    mid3, parts[3] = conv(3, parts, ((3, 0),))
    decoded = upsample(mid0, (0,))
    decoded = upsample(mid3, (3,), decoded)
    (late,) = conv(2, parts, ((1, 2), (2, 3)))
    decoded = upsample(late, (1, 2), decoded)
    return decoded.transpose(0, 2, 1, 3)


def solution(mesh):
    in_specs = (
        P("tile", ("groups", "seq"), "chan"),
        P(),
        P(None, None, None, None, "chan"),
        P("chan"),
        P(None, None, None, "chan"),
        P("chan"),
    )
    out_specs = P(None, ("groups", "tile"), "seq", "chan")
    return jax.shard_map(block_body, mesh=mesh, in_specs=in_specs, out_specs=out_specs, check_vma=False)
```

```python
import functools

import jax
import jax.numpy as jnp
from jax import lax
from jax.experimental import pallas as pl
from jax.experimental.pallas import tpu as pltpu
from jax.sharding import PartitionSpec as P


FRAMES = 8
ROWS_DEV = 24
PAIRS = FRAMES // 2
AHEAD = 2
PITCH = 32
HEAD = 8

norm_eps = 1e-06
f32 = jnp.float32
bf16 = jnp.bfloat16
VM = pl.BlockSpec(memory_space=pltpu.VMEM)
ANY = pl.BlockSpec(memory_space=pl.ANY)
MIB = 1024 * 1024


def dot_nt(a, b):
    return lax.dot_general(a, b, (((1,), (1,)), ((), ())), preferred_element_type=f32)


def call(kernel, out_shape, in_specs, out_specs, scratch, limit, flops=0, moved=0, aliases=None):
    return pl.pallas_call(
        kernel,
        out_shape=out_shape,
        in_specs=in_specs,
        out_specs=out_specs,
        scratch_shapes=list(scratch),
        compiler_params=pltpu.CompilerParams(vmem_limit_bytes=limit * MIB),
        input_output_aliases=aliases or {},
        cost_estimate=pl.CostEstimate(flops=flops, bytes_accessed=moved, transcendentals=0),
    )


def round_up(n, k):
    return -(-n // k) * k


def border_rows(width):
    return round_up(2 * width, 8)


def selection(rows, per_col, width, cols, span, dest, tokens):
    r = lax.broadcasted_iota(jnp.int32, (rows, 1), 0)
    w = jnp.zeros_like(r)
    for k in range(1, width):
        w = w + (r >= k * per_col).astype(jnp.int32)
    h = r - w * per_col
    col = dest * cols - 2 + w
    good = (col >= 0) & (col < span) & (r < width * per_col)
    token = jnp.where(good, h * span + col, -1)
    lane = lax.broadcasted_iota(jnp.int32, (rows, tokens), 1)
    return jnp.where(lane == token, 1.0, 0.0).astype(bf16)


def edge_kernel(span, colors, x_ref, *rest):
    here_ref, outs = rest[0], rest[1:]
    tile = lax.axis_index("tile")
    half = ROWS_DEV * span
    seg = round_up(2 * span, 64)
    chan = x_ref.shape[0]
    here_ref[...] = x_ref[...]
    for color in range(colors):
        below = lax.rem(tile + color, 2) == 0
        parts = []
        for p in range(2):
            last = here_ref[:, (p + 1) * half - 2 * span : (p + 1) * half]
            first = here_ref[:, p * half : p * half + 2 * span]
            parts += [jnp.where(below, last, first), jnp.zeros((chan, seg - 2 * span), bf16)]
        outs[color][...] = jnp.concatenate(parts, axis=1)


def pack_kernel(count, cols, x_ref, *outs):
    seq = lax.axis_index("seq")
    width, span = cols + 4, count * cols
    half = ROWS_DEV * span
    rows = width * ROWS_DEV
    for d in range(count):
        pick = selection(rows, ROWS_DEV, width, cols, span, jnp.bitwise_xor(seq, d), half)
        both = jnp.concatenate([dot_nt(pick, x_ref[:, p * half : (p + 1) * half]) for p in range(2)], axis=1)
        outs[d][0:rows, :] = both.astype(bf16)


def border_kernel(count, cols, colors, *refs):
    late = [d for d in range(count) if d != AHEAD]
    edges = refs[:colors]
    outs = refs[colors + len(late) : colors + 2 * len(late)]
    ahead_ref, held, sems = refs[colors + 2 * len(late) :]
    seq = lax.axis_index("seq")
    width, span = cols + 4, count * cols
    rows = border_rows(width)
    seg = round_up(2 * span, 64)
    picks = [selection(rows, 2, width, cols, span, jnp.bitwise_xor(seq, d), seg) for d in range(count)]
    pick = jnp.concatenate(picks, axis=0)
    for color in range(colors):
        x = edges[color][...]
        both = jnp.concatenate([dot_nt(pick, x[:, p * seg : (p + 1) * seg]) for p in range(2)], axis=1)
        for d in range(count):
            piece = both[d * rows : (d + 1) * rows].astype(bf16)
            if d == AHEAD:
                ahead_ref[color * rows : (color + 1) * rows, :] = piece
            else:
                held[late.index(d), color * rows : (color + 1) * rows, :] = piece
    copies = []
    for k in range(len(late)):
        to = outs[k].at[pl.ds(width * ROWS_DEV, colors * rows)]
        copies.append(pltpu.make_async_copy(held.at[k], to, sems.at[k]))
        copies[-1].start()
    for copy in copies:
        copy.wait()


def conv_kernel(cfg, *refs):
    width, kinds, ring, d, pieces = cfg
    gain_ref, w_ref, bias_ref = refs[:3]
    mine_refs, their_refs = refs[3 : 3 + pieces], refs[3 + pieces : 3 + 2 * pieces]
    refs = refs[3 + 2 * pieces :]
    before = {1: 1, 3: 3}.get(d, 0)
    parts = list(refs[:before])
    rest = refs[before:]
    pad_ref, raw_ref, lhs_ref = rest[-3:]
    mid_ref = rest[0] if d in (1, 3) else None
    part_ref = rest[1] if d in (1, 3) else rest[0]
    parts.append(part_ref)
    tile, chan_id, tiles = lax.axis_index("tile"), lax.axis_index("chan"), lax.axis_size("tile")
    seq, seqs = lax.axis_index("seq"), lax.axis_size("seq")
    chan = gain_ref.shape[0] // 2
    out_rows = (width - 2) * PITCH
    gain = gain_ref[...].reshape(1, 2 * chan)
    pad_ref[...] = jnp.zeros_like(pad_ref)
    raw_ref[...] = jnp.zeros_like(raw_ref)
    main = width * ROWS_DEV

    def place(raw, act, first):
        for w in range(width):
            to = slice(w * PITCH + first, w * PITCH + first + 2)
            pad_ref[to, :] = act[2 * w : 2 * w + 2]
            raw_ref[to, :] = raw[2 * w : 2 * w + 2]

    for p in range(2):
        lanes = slice(p * chan, (p + 1) * chan)
        mine = jnp.concatenate([ref[:, lanes].astype(f32) for ref in mine_refs], axis=0)
        theirs = jnp.concatenate([ref[:, lanes].astype(f32) for ref in their_refs], axis=0)
        low = jnp.where(chan_id == 0, mine, theirs)
        high = jnp.where(chan_id == 0, theirs, mine)
        x = jnp.concatenate([low, high], axis=1)
        scale = lax.rsqrt(jnp.mean(x * x, axis=-1, keepdims=True) + norm_eps)
        v = x * scale * gain
        act = v / (1.0 + jnp.exp(-v))
        raw = mine
        for w in range(width):
            to = slice(w * PITCH + HEAD, w * PITCH + HEAD + ROWS_DEV)
            pad_ref[to, :] = act[w * ROWS_DEV : (w + 1) * ROWS_DEV]
            raw_ref[to, :] = raw[w * ROWS_DEV : (w + 1) * ROWS_DEV]
        tops, bottoms = [], []
        for k, kind in enumerate(kinds):
            at = main + k * border_rows(width)
            cells = raw[at : at + 2 * width], act[at : at + 2 * width]
            if kind == "top":
                tops.append(cells)
            elif kind == "bottom":
                bottoms.append(cells)
            else:
                below = lax.rem(tile + int(kind), 2) == 0
                tops.append([jnp.where(below, 0.0, cell) for cell in cells])
                bottoms.append([jnp.where(below, cell, 0.0) for cell in cells])
        for found, first in ((tops, HEAD - 2), (bottoms, HEAD + ROWS_DEV)):
            if found:
                place(functools.reduce(jnp.add, [f[0] for f in found]), functools.reduce(jnp.add, [f[1] for f in found]), first)
        for dh in range(3):
            shifted = pad_ref[HEAD - 2 + dh : HEAD - 2 + dh + width * PITCH, :]
            lhs_ref[p, :, dh * 2 * chan : (dh + 1) * 2 * chan] = shifted.astype(bf16)
        part_ref[p] = raw_ref[PITCH + HEAD - 1 : PITCH + HEAD - 1 + out_rows, :]

    lhs = jnp.concatenate(
        [lhs_ref[:, dw * PITCH : dw * PITCH + out_rows, :].reshape(2 * out_rows, 6 * chan) for dw in range(3)], axis=1
    )
    zero = jnp.zeros((out_rows, chan), f32)
    for dt in (2, 1, 0):
        taps = [w_ref[dt * 9 + dh * 3 + dw] for dw in range(3) for dh in range(3)]
        total = dot_nt(lhs, jnp.concatenate(taps, axis=1)).reshape(2, out_rows, chan)
        if dt == 2:
            part_ref[0] += total[0]
            part_ref[1] += total[1]
        elif dt == 1:
            part_ref[1] += total[0]
            part_ref[2] = total[1]
        else:
            part_ref[2] += total[0]
            part_ref[3] = total[1]

    if d in (1, 3):
        r = lax.broadcasted_iota(jnp.int32, (out_rows, 1), 0)
        h = jnp.bitwise_and(r, PITCH - 1) - 1
        good = (h >= jnp.where(tile == 0, 0, -1)) & (h < jnp.where(tile == tiles - 1, ROWS_DEV, ROWS_DEV + 1))
        good = good & (r >= jnp.where(seq == 0, PITCH, 0)) & (r < jnp.where(seq == seqs - 1, out_rows - PITCH, out_rows))
        base = seq if ring else 0
        odd = lax.rem(base, 2) == 1
        high = base >= PAIRS // 2

        def part(k, n):
            pair = (parts[k - k % 2][n], parts[k - k % 2 + 1][n])
            return jnp.where(odd, pair[1 - k % 2], pair[k % 2])

        for k, pair in enumerate(((1,),) if d == 1 else ((0,), (2,), (3,))):
            mids = []
            for p in range(2):
                value = part(pair[0], p) + bias_ref[...]
                if pair[0] % 2:
                    value = value + part(pair[0] - 1, 2 + p)
                elif pair[0] == 0:
                    value = value + jnp.where(high, part(3, 2 + p), 0.0)
                else:
                    value = value + jnp.where(high, 0.0, part(1, 2 + p))
                mids.append(jnp.where(good, value, 0.0))
            mid_ref[k] = jnp.concatenate(mids, axis=1).astype(bf16)


def tap_kernel(w_ref, bias_ref, out_ref, wide_ref, rows_ref):
    out_chan, chans = w_ref.shape[1:]
    lane = lax.broadcasted_iota(jnp.int32, (out_chan, wide_ref.shape[1]), 1)
    row = lax.broadcasted_iota(jnp.int32, lane.shape, 0)
    spread = jnp.where((lane == 2 * row) | (lane == 2 * row + 1), 1.0, 0.0)
    dims = (((1,), (0,)), ((), ()))
    wide_ref[...] = lax.dot_general(bias_ref[...], spread, dims, precision=lax.Precision.HIGHEST, preferred_element_type=f32)
    rows_ref[...] = jnp.zeros_like(rows_ref)
    taps = [[w_ref[dr * 3 + ds].astype(f32) for ds in range(3)] for dr in range(3)]
    by_row = [[[taps[0][s] for s in range(3)], [taps[1][s] + taps[2][s] for s in range(3)]]]
    by_row.append([[taps[0][s] + taps[1][s] for s in range(3)], [taps[2][s] for s in range(3)]])
    for i in range(2):
        for dw in range(3):
            for a in range(2):
                t = by_row[i][a]
                zero = jnp.zeros_like(t[0])
                left = (t[0], t[1] + t[2], zero)[dw]
                right = (zero, t[0] + t[1], t[2])[dw]
                for k in range(chans // 128):
                    lanes = slice(k * 128, (k + 1) * 128)
                    rows_ref[pl.ds(0, out_chan, stride=2), :] = left[:, lanes]
                    rows_ref[pl.ds(1, out_chan, stride=2), :] = right[:, lanes]
                    to = a * chans + k * 128
                    out_ref[i, dw, :, to : to + 128] = rows_ref[...].astype(bf16)


def up_kernel(cfg, *refs):
    mid_w, ring, final = cfg
    own_ref, other_ref, w_ref, bias_ref = refs[:4]
    if final:
        first_ref, out_ref, lhs_ref, rows_ref, held_ref, sems = refs[4:]
    else:
        held_ref, lhs_ref, rows_ref = refs[4:]
    chan_id = lax.axis_index("chan")
    copies = []

    def write(source, pair, sem):
        base = lax.axis_index("seq") if ring else 0
        half = jnp.where(base >= PAIRS // 2, PAIRS // 2, 0)
        frame = 2 * (half + pair if pair < 2 else PAIRS // 2 - half + pair - 2)
        copies.append(pltpu.make_async_copy(source, out_ref.at[pl.ds(frame, 2)], sem))
        copies[-1].start()

    if final:
        write(first_ref, 1, sems.at[0])
    chan = own_ref.shape[2] // 2
    cols = mid_w - 2
    keep = (mid_w - 1) * PITCH + ROWS_DEV
    count = own_ref.shape[0]
    frames = 2 * count
    lanes = w_ref.shape[2]
    span = cols * PITCH
    lhs_ref[:, keep:, :] = jnp.zeros_like(lhs_ref[:, keep:, :])
    for k in range(count):
        for p in range(2):
            mine = own_ref[k, :, p * chan : (p + 1) * chan]
            theirs = other_ref[k, :, p * chan : (p + 1) * chan]
            low = jnp.where(chan_id == 0, mine, theirs)
            high = jnp.where(chan_id == 0, theirs, mine)
            x = jnp.concatenate([low, high], axis=1).astype(f32)
            for a in range(3):
                lhs_ref[2 * k + p, 0:keep, a * 2 * chan : (a + 1) * 2 * chan] = x[a : a + keep].astype(bf16)
    for i in range(2):
        lhs = jnp.concatenate(
            [
                lhs_ref[:, dw * PITCH : dw * PITCH + span, i * 2 * chan : (i + 2) * 2 * chan].reshape(frames * span, 4 * chan)
                for dw in range(3)
            ],
            axis=1,
        )
        total = dot_nt(lhs, jnp.concatenate([w_ref[i, dw] for dw in range(3)], axis=1))
        total = total.reshape(frames, span, lanes)
        for f in range(frames):
            for w in range(cols):
                for k in range(lanes // 128):
                    piece = total[f, w * PITCH : w * PITCH + ROWS_DEV, k * 128 : (k + 1) * 128]
                    rows_ref[k, f * cols + w, pl.ds(i, ROWS_DEV, stride=2), :] = piece
    bias = bias_ref[:, : held_ref.shape[3]]
    for k in range(count):
        for f in (2 * k, 2 * k + 1):
            for w in range(cols):
                row = jnp.concatenate([rows_ref[c, f * cols + w] for c in range(lanes // 128)], axis=1)
                held_ref[f, w] = (row[:, : held_ref.shape[3]] + bias).astype(bf16)
        if final:
            write(held_ref.at[pl.ds(2 * k, 2)], (0, 2, 3)[k], sems.at[1 + k])
    for copy in copies:
        copy.wait()


def swap_chan(x):
    return lax.ppermute(x, "chan", [(0, 1), (1, 0)])


def tile_pairs(color, tiles):
    out = []
    for t in range(color, tiles - 1, 2):
        out += [(t, t + 1), (t + 1, t)]
    return out


def arrive_by_trade(latents, cols):
    seqs, tiles = lax.axis_size("seq"), lax.axis_size("tile")
    colors = min(2, tiles - 1)
    width, span = cols + 4, cols * seqs
    chan = latents.shape[2]
    x = latents[0].T
    border = border_rows(width)
    rows = width * ROWS_DEV + colors * border
    edge = jax.ShapeDtypeStruct((chan, 2 * round_up(2 * span, 64)), bf16)
    block = jax.ShapeDtypeStruct((rows, 2 * chan), bf16)
    whole = jax.ShapeDtypeStruct(x.shape, bf16)
    bare = jax.ShapeDtypeStruct((width * ROWS_DEV, 2 * chan), bf16)
    outs = [bare if d == AHEAD else block for d in range(seqs)]
    late = [d for d in range(seqs) if d != AHEAD]
    here, *edges = call(
        functools.partial(edge_kernel, span, colors), [whole] + [edge] * colors, [VM], [VM] * (1 + colors), [], 4
    )(x)
    windows = call(functools.partial(pack_kernel, seqs, cols), outs, [VM], [VM] * seqs, [], 12, flops=2 * 10**9)(here)
    edges = [lax.ppermute(e, "tile", tile_pairs(color, tiles)) for color, e in enumerate(edges)]
    *done, borders = call(
        functools.partial(border_kernel, seqs, cols, colors),
        [block] * len(late) + [jax.ShapeDtypeStruct((colors * border, 2 * chan), bf16)],
        [VM] * colors + [ANY] * len(late),
        [ANY] * len(late) + [VM],
        [pltpu.VMEM((len(late), colors * border, 2 * chan), bf16), pltpu.SemaphoreType.DMA((len(late),))],
        4,
        aliases={colors + k: k for k in range(len(late))},
    )(*edges, *[windows[d] for d in late])

    def trade(x, d):
        return lax.ppermute(x, "seq", [(i, i ^ d) for i in range(seqs)])

    blocks = [(done[0],)]
    for d in range(1, seqs):
        blocks.append((trade(windows[d], d), trade(borders, d)) if d == AHEAD else (trade(done[late.index(d)], d),))
    return blocks, [str(c) for c in range(colors)]


def extended(cells, sides, width):
    for axis, dim in sides:
        count = lax.axis_size(axis)
        ends = count - 1
        head = lax.slice_in_dim(cells, 0, width, axis=dim)
        tail = lax.slice_in_dim(cells, cells.shape[dim] - width, cells.shape[dim], axis=dim)
        cells = jnp.concatenate(
            [
                lax.ppermute(tail, axis, [(i, (i + 1) % count) for i in range(ends)]),
                cells,
                lax.ppermute(head, axis, [((i + 1) % count, i) for i in range(ends)]),
            ],
            axis=dim,
        )
    return cells


def arrive_by_all_to_all(latents, cols):
    seqs = lax.axis_size("seq")
    chan = latents.shape[2]
    width = cols + 4
    arranged = latents[0].reshape(FRAMES * ROWS_DEV // seqs, seqs, cols, chan)
    regrouped = lax.all_to_all(arranged, "seq", split_axis=1, concat_axis=0, tiled=True)
    field = regrouped.reshape(FRAMES, ROWS_DEV, cols, chan)
    field = extended(field, (("seq", 2), ("tile", 1)), 2)
    paired = field.reshape(PAIRS, 2, ROWS_DEV + 4, width, chan).transpose(0, 3, 2, 1, 4)
    paired = paired.reshape(PAIRS, width, ROWS_DEV + 4, 2 * chan)
    spare = ((0, border_rows(width) - 2 * width), (0, 0))
    blocks = []
    for d in range(PAIRS):
        pieces = [paired[d, :, 2:-2].reshape(-1, 2 * chan)]
        pieces += [jnp.pad(b.reshape(-1, 2 * chan), spare) for b in (paired[d, :, :2], paired[d, :, -2:])]
        blocks.append((jnp.concatenate(pieces, axis=0),))
    return blocks, ["top", "bottom"]


def block_body(latents, norm_gain, conv_weight, conv_bias, upsample_weight, upsample_bias):
    chan, out_chan = conv_bias.shape[0], upsample_bias.shape[0]
    cols = latents.shape[1] // (FRAMES * ROWS_DEV)
    width, mid_w = cols + 4, cols + 2
    out_rows = mid_w * PITCH
    ring = 2 * lax.axis_size("seq") == FRAMES
    blocks, kinds = arrive_by_trade(latents, cols) if ring else arrive_by_all_to_all(latents, cols)

    up_lanes = round_up(2 * out_chan, 128)
    taps = upsample_weight.transpose(0, 1, 3, 2).reshape(9, out_chan, 2 * chan)
    up_weights, up_bias = call(
        tap_kernel,
        [jax.ShapeDtypeStruct((2, 3, up_lanes, 4 * chan), bf16), jax.ShapeDtypeStruct((1, up_lanes), f32)],
        [VM, VM],
        [VM, VM],
        [pltpu.VMEM((up_lanes, 128), f32)],
        12,
        flops=10**9,
    )(taps, upsample_bias[None])

    weights = conv_weight.transpose(0, 1, 2, 4, 3).reshape(27, chan, 2 * chan)
    gain, bias = norm_gain, conv_bias[None]
    part = jax.ShapeDtypeStruct((4, out_rows, chan), f32)
    work = [
        pltpu.VMEM((width * PITCH + 2 * HEAD, 2 * chan), f32),
        pltpu.VMEM((width * PITCH + 2 * HEAD, chan), f32),
        pltpu.VMEM((2, width * PITCH, 6 * chan), bf16),
    ]

    def conv(d, *before):
        outs = [jax.ShapeDtypeStruct((d, out_rows, 2 * chan), bf16)] if d in (1, 3) else []
        outs += [part] if d < 3 else []
        others = [swap_chan(block) for block in blocks[d]]
        return call(
            functools.partial(conv_kernel, (width, kinds, ring, d, len(others))),
            outs,
            [VM] * (3 + 2 * len(others) + len(before)),
            [VM] * len(outs),
            ([] if d < 3 else [pltpu.VMEM((4, out_rows, chan), f32)]) + work,
            14,
            flops=2 * 2 * out_rows * 27 * 2 * chan * 256,
        )(gain, weights, bias, *blocks[d], *others, *before)

    def upsample(mids, *early):
        count, final = mids.shape[0], len(early)
        held = (2 * count, cols, 2 * ROWS_DEV, 2 * out_chan)
        scratch = [
            pltpu.VMEM((2 * count, out_rows, 6 * chan), bf16),
            pltpu.VMEM((up_lanes // 128, 2 * count * cols, 2 * ROWS_DEV, 128), f32),
        ]
        if final:
            scratch += [pltpu.VMEM(held, bf16), pltpu.SemaphoreType.DMA((1 + count,))]
        other = swap_chan(mids)
        return call(
            functools.partial(up_kernel, (mid_w, ring, final)),
            jax.ShapeDtypeStruct((FRAMES, *held[1:]) if final else held, bf16),
            [VM] * (4 + final),
            ANY if final else VM,
            scratch,
            14,
            flops=2 * 2 * 2 * count * cols * PITCH * 12 * chan * 256,
        )(mids, other, up_weights, up_bias, *early)

    (part0,) = conv(0)
    early, part1 = conv(1, part0)
    first = upsample(early)
    (part2,) = conv(2)
    (late,) = conv(3, part0, part1, part2)
    return upsample(late, first).transpose(0, 2, 1, 3)


def solution(mesh):
    in_specs = (
        P("tile", ("groups", "seq"), "chan"),
        P(),
        P(None, None, None, None, "chan"),
        P("chan"),
        P(None, None, None, "chan"),
        P("chan"),
    )
    out_specs = P(None, ("groups", "tile"), "seq", "chan")
    return jax.shard_map(block_body, mesh=mesh, in_specs=in_specs, out_specs=out_specs, check_vma=False)
```
